32 devices in a mesh: dp: 16 (over z, y, x), mp: 2 (over core).
Axes of the slice: x: 2, y: 2, z: 4, core: 2. Of those that a mesh axis runs over, the one named last changes fastest.
Arguments:
- store_rows: bfloat16 [8192, 4096], P('dp', 'mp'), may hold values from -64 to 64
- norm_gain: bfloat16 [4096], replicated, may hold values from 0.099609375 to 1.8984375
- key_weight: bfloat16 [4096, 2048], P(None, 'mp'), may hold values from -0.09375 to 0.09375
- value_weight: bfloat16 [4096, 2048], P(None, 'mp'), may hold values from -0.09375 to 0.09375
- queries: bfloat16 [128, 2048], P('dp', 'mp'), may hold values from -300 to 300
- counts: int32 [16], replicated, may hold values from 1 to 8, 32 in all
- slot_plan: int32 [32], P('dp'), may hold values from 0 to 31, each once
Outputs:
- context: bfloat16 [128, 2048], P('dp', 'mp')
The draws below stay inside these ranges and needn't reach their ends.
All inputs are finite; a program needn't handle non-finite values.
Results may differ from the reference program's by a relative error of at most 0.0091.
Values may be sent and summed in bfloat16 or wider, within the bound.
A program may use at most 64 MiB of HBM per device.

```python
import math
import jax
import jax.numpy as jnp
import numpy as np
from jax import lax

D = 4096
HEADS = 32
HEAD_DIM = 64
PASSAGE_LEN = 256
MOST = 8
DEC = 8
QUESTIONS = 16
PASSAGES = 32


def draw_store_rows(key, part):
    first_key, second_key, third_key = jax.random.split(key, 3)
    row_total = PASSAGES * PASSAGE_LEN
    column_pos = jnp.arange(D, dtype=jnp.float32) / D
    column_scale = 0.5 * jnp.power(3.0, column_pos) * jnp.exp(jax.random.uniform(second_key, (D,), jnp.float32, -0.35, 0.35))
    row_scale = jnp.exp(jax.random.uniform(third_key, (row_total, 1), jnp.float32, 0.0, math.log(10.0)))
    base_rows = jax.random.normal(first_key, (row_total, D), jnp.float32)
    return jnp.clip(base_rows * row_scale * column_scale[None, :], -64.0, 64.0).astype(jnp.bfloat16)


def draw_queries(key, part):
    first_key = jax.random.fold_in(key, 0)
    row_total = QUESTIONS * DEC
    column_total = HEADS * HEAD_DIM
    base_rows = jax.random.normal(first_key, (row_total, column_total), jnp.float32) * 2.5
    return jnp.clip(base_rows, -300.0, 300.0).astype(jnp.bfloat16)


def levels(rng, shape, cuts, smallest, high):
    def one(axis_at, parts):
        heights = jax.random.uniform(jax.random.fold_in(jax.random.fold_in(rng, 6), axis_at), (parts,), jnp.float32, smallest / len(cuts), high / len(cuts))
        return jnp.repeat(jnp.exp(heights), shape[axis_at] // parts).reshape((-1,) + (1,) * (len(shape) - axis_at - 1))

    level = one(*cuts[0])
    for cut in cuts[1:]:
        level = level * one(*cut)
    return level


def length_profile(count, total, most, skew):
    weights = [(1 << 20) // math.isqrt(grade ** skew) + 1 for grade in range(2, count + 1)]
    spare, holding = total - most - (count - 1), [1] * (count - 1)
    while spare > 0:
        movable = [i for i in range(count - 1) if holding[i] < most]
        pool, left = sum([weights[i] for i in movable]), spare
        for i in movable:
            addition = min(most - holding[i], max(1, left * weights[i] // pool), spare)
            holding[i] = holding[i] + addition
            spare = spare - addition
    return np.array([most] + holding)


def uneven(own_key, count, total, most, lean):
    if count == 2:
        one = jax.random.randint(own_key, (), max(1, total - most), min(most, total - 1) + 1)
        return jnp.stack([one, total - one])
    sizes = jnp.asarray(length_profile(count, total, most, lean), jnp.int32)
    pairs = (count - 1) // 2
    donor, receiver = sizes[1:1 + 2 * pairs:2], sizes[2:2 + 2 * pairs:2]
    room = jnp.minimum(donor - 1, most - receiver)
    passed = jax.random.randint(jax.random.fold_in(own_key, 1), (pairs,), 0, 1 << 20) % (room + 1)
    sizes = sizes.at[1:1 + 2 * pairs:2].set(donor - passed).at[2:2 + 2 * pairs:2].set(receiver + passed)
    return sizes[jax.random.permutation(jax.random.fold_in(own_key, 2), count)]


def normal_values(key, extent, spread, reach, cuts=(), kind=jnp.bfloat16):
    result = spread * jax.random.normal(key, extent, jnp.float32)
    if cuts:
        result = result * levels(key, extent, cuts, -0.22, 0.18)
    return jnp.clip(result, -reach, reach).astype(kind)


def setup_inputs(seed: int = 0) -> dict:
    keys = jax.random.split(jax.random.key(seed), 8)
    return {
        "store_rows": draw_store_rows(jax.random.fold_in(keys[7], 71), 0),
        "norm_gain": jnp.clip(1.0 + 0.18 * jax.random.normal(keys[1], (D,), jnp.float32), 0.099609375, 1.8984375).astype(jnp.bfloat16),
        "key_weight": normal_values(keys[2], (D, HEADS * HEAD_DIM), D ** -0.5, 0.09375, ((1, 2),)),
        "value_weight": normal_values(keys[3], (D, HEADS * HEAD_DIM), D ** -0.5, 0.09375, ((1, 2),)),
        "queries": draw_queries(jax.random.fold_in(keys[7], 71), 0),
        "counts": uneven(keys[5], QUESTIONS, PASSAGES, MOST, 2).astype(jnp.int32),
        "slot_plan": jax.random.permutation(keys[6], PASSAGES).astype(jnp.int32),
    }


norm_eps = 1e-06
score_scale = 0.125
far_below = -1e+30

def reference(store_rows, norm_gain, key_weight, value_weight, queries, counts, slot_plan):
    row_blocks = store_rows.reshape(PASSAGES, PASSAGE_LEN, D)
    gain_full = norm_gain.astype(jnp.float32)

    def project(row_block):
        raw_rows = row_block.astype(jnp.float32)
        inv_rms = lax.rsqrt(lax.optimization_barrier(jnp.mean(raw_rows * raw_rows, axis=1, keepdims=True)) + norm_eps)
        scaled = (raw_rows * gain_full[None, :]).astype(jnp.bfloat16)
        key_rows = (jnp.dot(scaled, key_weight, preferred_element_type=jnp.float32) * inv_rms).astype(jnp.bfloat16)
        value_rows = (jnp.dot(scaled, value_weight, preferred_element_type=jnp.float32) * inv_rms).astype(jnp.bfloat16)
        return (key_rows, value_rows)
    all_keys, all_values = lax.map(project, row_blocks)
    ends = jnp.cumsum(counts)
    slot_question = lax.optimization_barrier(jnp.sum((slot_plan[:, None] >= ends[None, :]).astype(jnp.int32), axis=1))
    query_table = queries.reshape(QUESTIONS, DEC, HEADS, HEAD_DIM)

    def scores_of(key_block, question):
        own_queries = jnp.take(query_table, question, axis=0).astype(jnp.float32)
        key_heads = key_block.reshape(PASSAGE_LEN, HEADS, HEAD_DIM).astype(jnp.float32)
        return jnp.einsum('ihd,thd->hit', own_queries, key_heads, precision=lax.Precision.HIGHEST) * score_scale

    def slot_peak(slot_item):
        return lax.optimization_barrier(jnp.max(scores_of(slot_item[0], slot_item[1]), axis=2))
    slot_max = lax.map(slot_peak, (all_keys, slot_question))
    member = slot_question[None, :] == jnp.arange(QUESTIONS, dtype=jnp.int32)[:, None]
    question_max = lax.optimization_barrier(jnp.max(jnp.where(member[:, :, None, None], slot_max[None], far_below), axis=1))

    def slot_terms(slot_item):
        key_block, value_block, question = slot_item
        scores = scores_of(key_block, question)
        weights = jnp.exp(scores - question_max[question][:, :, None])
        value_heads = value_block.reshape(PASSAGE_LEN, HEADS, HEAD_DIM).astype(jnp.float32)
        slot_num = jnp.einsum('hit,thd->hid', weights, value_heads, precision=lax.Precision.HIGHEST)
        return (slot_num, lax.optimization_barrier(jnp.sum(weights, axis=2)))
    slot_num, slot_den = lax.map(slot_terms, (all_keys, all_values, slot_question))
    numerator = jax.ops.segment_sum(slot_num, slot_question, num_segments=QUESTIONS)
    denominator = jax.ops.segment_sum(slot_den, slot_question, num_segments=QUESTIONS)
    context = numerator / denominator[..., None]
    return jnp.transpose(context, (0, 2, 1, 3)).reshape(QUESTIONS * DEC, HEADS * HEAD_DIM).astype(jnp.bfloat16)
```

```python
import functools

import jax
import jax.numpy as jnp
from jax import lax
from jax.experimental import pallas as pl
from jax.experimental.pallas import tpu as pltpu
from jax.sharding import PartitionSpec as P

HEAD_DIM = 64
MESH = pl.DeviceIdType.MESH

norm_eps = 1e-06
score_scale = 0.125
far_below = -1e30


def body(dims, counts, plan, gain, queries, rows_hbm, key_hbm, value_hbm, out,
         raw, scaled, wbuf, acc, kvb, sumsq, qbuf, part, stat, sbuf, rbuf,
         rows_sem, w_sem, rsend, rrecv, qsend, qrecv, osend, orecv):
    dp, mp, row_count, feats, cols, width, questions, dec, passages = dims
    full = feats * mp
    seq = row_count // passages
    groups = cols // width
    chunks = 2 * groups
    heads = cols // HEAD_DIM
    gheads = width // HEAD_DIM
    me = lax.axis_index("dp")
    core = lax.axis_index("mp")

    own_rows = pltpu.make_async_copy(rows_hbm, raw.at[0], rows_sem)
    own_rows.start()

    def weight_copy(s, c):
        owner = lax.rem(core + s, mp)
        source = key_hbm if c < groups else value_hbm
        at = (c % groups) * width
        return pltpu.make_async_copy(
            source.at[pl.ds(pl.multiple_of(owner * feats, feats), feats), pl.ds(at, width)],
            wbuf.at[s, c], w_sem.at[s, c])

    for s in range(mp):
        for c in range(chunks):
            weight_copy(s, c).start()

    barrier = pltpu.get_barrier_semaphore()
    for j in range(1, dp):
        pl.semaphore_signal(barrier, inc=1, device_id=(lax.rem(me + j, dp), core), device_id_type=MESH)
    for s in range(1, mp):
        pl.semaphore_signal(barrier, inc=1, device_id=(me, lax.rem(core + s, mp)), device_id_type=MESH)
    pl.semaphore_wait(barrier, dp - 1 + mp - 1)

    row_copies = []
    for s in range(1, mp):
        row_copies.append(pltpu.make_async_remote_copy(
            src_ref=rows_hbm, dst_ref=raw.at[s], send_sem=rsend.at[s], recv_sem=rrecv.at[s],
            device_id=(me, lax.rem(core + mp - s, mp)), device_id_type=MESH))
        row_copies[-1].start()
    query_copies = []
    for j in range(1, dp):
        query_copies.append(pltpu.make_async_remote_copy(
            src_ref=queries, dst_ref=qbuf.at[me], send_sem=qsend.at[j], recv_sem=qrecv.at[j],
            device_id=(lax.rem(me + j, dp), core), device_id_type=MESH))
        query_copies[-1].start()
    qbuf[me] = queries[...]

    row_step = 64

    def scale(s):
        owner = lax.rem(core + s, mp)
        own_gain = gain[:, pl.ds(pl.multiple_of(owner * feats, feats), feats)].astype(jnp.float32)

        def step(i, carry):
            at = pl.ds(pl.multiple_of(i * row_step, row_step), row_step)
            x = raw[s, at, :].astype(jnp.float32)
            scaled[s, at, :] = (x * own_gain).astype(jnp.bfloat16)
            total = jnp.sum(x * x, axis=1, keepdims=True)
            if s > 0:
                total = total + sumsq[at, :]
            sumsq[at, :] = total
            return carry

        lax.fori_loop(0, row_count // row_step, step, 0)

    own_rows.wait()
    for s in range(mp):
        if s > 0:
            row_copies[s - 1].wait()
        scale(s)
        if s == mp - 1:
            inv_rms = lax.rsqrt(sumsq[...] * (1.0 / full) + norm_eps)
        for c in range(chunks):
            weight_copy(s, c).wait()
            product = jnp.dot(scaled[s], wbuf[s, c], preferred_element_type=jnp.float32)
            if s > 0:
                product = product + acc[c]
            if s == mp - 1:
                kvb[c] = (product * inv_rms).astype(jnp.bfloat16)
            else:
                acc[c] = product

    for copy in query_copies:
        copy.wait()

    slot = []
    for p in range(passages):
        plan_p = plan[p]

        def count(q, carry):
            end, total = carry
            end = end + counts[q]
            return end, total + jnp.where(end <= plan_p, 1, 0)

        found = lax.fori_loop(0, questions, count, (jnp.int32(0), jnp.int32(0)))[1]
        slot.append(jnp.minimum(found, questions - 1))
    same = [[slot[a] == slot[b] for b in range(passages)] for a in range(passages)]

    tall = gheads * dec
    row_head = lax.broadcasted_iota(jnp.int32, (tall, width), 0) // dec
    col_head = lax.broadcasted_iota(jnp.int32, (tall, width), 1) // HEAD_DIM
    diagonal = row_head == col_head
    stat_row = lax.broadcasted_iota(jnp.int32, (tall, 128), 0) // dec
    stat_lane = lax.broadcasted_iota(jnp.int32, (tall, 128), 1)
    own_queries = [qbuf[slot[p]].astype(jnp.float32) for p in range(passages)]

    stats = [jnp.zeros((dec, 128), jnp.float32) for _ in range(passages)]
    for g in range(groups):
        scores, tops = [], []
        for p in range(passages):
            q = own_queries[p][:, g * width:(g + 1) * width]
            q = jnp.where(diagonal, jnp.concatenate([q] * gheads, axis=0), 0.0).astype(jnp.bfloat16)
            k = kvb[g, p * seq:(p + 1) * seq, :]
            s = lax.dot_general(q, k, (((1,), (1,)), ((), ())), preferred_element_type=jnp.float32) * score_scale
            scores.append(s)
            tops.append(jnp.max(s, axis=1, keepdims=True))
        nums, dens, levels = [], [], []
        for p in range(passages):
            level = tops[p]
            for o in range(passages):
                if o != p:
                    level = jnp.maximum(level, jnp.where(same[p][o], tops[o], far_below))
            w = jnp.exp(scores[p] - level)
            dens.append(jnp.sum(w, axis=1, keepdims=True))
            v = kvb[groups + g, p * seq:(p + 1) * seq, :]
            nums.append(jnp.dot(w.astype(jnp.bfloat16), v, preferred_element_type=jnp.float32))
            levels.append(level)
        for p in range(passages):
            num, den = nums[p], dens[p]
            for o in range(passages):
                if o != p:
                    num = num + jnp.where(same[p][o], nums[o], 0.0)
                    den = den + jnp.where(same[p][o], dens[o], 0.0)
            o_group = jnp.where(diagonal, num / den, 0.0)
            part[p, :, g * width:(g + 1) * width] = jnp.sum(o_group.reshape(gheads, dec, width), axis=0)
            lse = jnp.broadcast_to(levels[p] + jnp.log(den), (tall, 128))
            head = stat_row + g * gheads
            put = (stat_lane == head) | (stat_lane == head + heads) | (stat_lane == head + 2 * heads)
            stats[p] = stats[p] + jnp.sum(jnp.where(put, lse, 0.0).reshape(gheads, dec, 128), axis=0)
    lane = lax.broadcasted_iota(jnp.int32, (dec, 128), 1)
    for p in range(passages):
        high = stats[p].astype(jnp.bfloat16).astype(jnp.float32)
        rest = stats[p] - high
        middle = rest.astype(jnp.bfloat16).astype(jnp.float32)
        low = rest - middle
        stat[p] = jnp.where(lane < heads, high, jnp.where(lane < 2 * heads, middle, low))
    nothing = jnp.where(lane < heads, far_below, 0.0)

    def payload(dst):
        a = jnp.zeros((dec, cols), jnp.float32)
        b = nothing
        for p in range(passages):
            a = jnp.where(slot[p] == dst, part[p], a)
            b = jnp.where(slot[p] == dst, stat[p], b)
        return a.astype(jnp.bfloat16), b.astype(jnp.bfloat16)

    out_copies = []
    for j in range(1, dp):
        dst = lax.rem(me + j, dp)
        a, b = payload(dst)
        sbuf[j, :, :cols] = a
        sbuf[j, :, cols:] = b
        out_copies.append(pltpu.make_async_remote_copy(
            src_ref=sbuf.at[j], dst_ref=rbuf.at[me], send_sem=osend.at[j], recv_sem=orecv.at[j],
            device_id=(dst, core), device_id_type=MESH))
        out_copies[-1].start()
    a, b = payload(me)
    rbuf[me, :, :cols] = a
    rbuf[me, :, cols:] = b
    for copy in out_copies:
        copy.wait()

    pick_row = lax.broadcasted_iota(jnp.int32, (128, width), 0)
    pick_col = lax.broadcasted_iota(jnp.int32, (128, width), 1) // HEAD_DIM
    got = rbuf[:, :, cols:].astype(jnp.float32).reshape(dp * dec, 128).astype(jnp.bfloat16)
    for g in range(groups):
        head = pick_col + g * gheads
        pick = (pick_row == head) | (pick_row == head + heads) | (pick_row == head + 2 * heads)
        pick = jnp.where(pick, 1.0, 0.0).astype(jnp.bfloat16)
        lse = jnp.dot(got, pick, preferred_element_type=jnp.float32).reshape(dp, dec, width)
        share = jnp.exp(lse - jnp.max(lse, axis=0, keepdims=True))
        parts = rbuf[:, :, g * width:(g + 1) * width].astype(jnp.float32)
        total = jnp.sum(share * parts, axis=0) / jnp.sum(share, axis=0)
        out[:, g * width:(g + 1) * width] = total.astype(jnp.bfloat16)


def local(dp, mp, store_rows, norm_gain, key_weight, value_weight, queries, counts, slot_plan):
    row_count, feats = store_rows.shape
    cols = key_weight.shape[1]
    width = min(256, cols)
    passages = slot_plan.shape[0]
    dec = queries.shape[0]
    questions = counts.shape[0]
    chunks = 2 * cols // width
    dims = (dp, mp, row_count, feats, cols, width, questions, dec, passages)
    vmem = pl.BlockSpec(memory_space=pltpu.VMEM)
    smem = pl.BlockSpec(memory_space=pltpu.SMEM)
    hbm = pl.BlockSpec(memory_space=pl.ANY)
    bf16, f32 = jnp.bfloat16, jnp.float32
    dma = pltpu.SemaphoreType.DMA
    return pl.pallas_call(
        functools.partial(body, dims),
        out_shape=jax.ShapeDtypeStruct((dec, cols), bf16),
        in_specs=[smem, smem, vmem, vmem, hbm, hbm, hbm],
        out_specs=vmem,
        scratch_shapes=[
            pltpu.VMEM((mp, row_count, feats), bf16),
            pltpu.VMEM((mp, row_count, feats), bf16),
            pltpu.VMEM((mp, chunks, feats, width), bf16),
            pltpu.VMEM((chunks, row_count, width), f32),
            pltpu.VMEM((chunks, row_count, width), bf16),
            pltpu.VMEM((row_count, 1), f32),
            pltpu.VMEM((dp, dec, cols), bf16),
            pltpu.VMEM((passages, dec, cols), f32),
            pltpu.VMEM((passages, dec, 128), f32),
            pltpu.VMEM((dp, dec, cols + 128), bf16),
            pltpu.VMEM((dp, dec, cols + 128), bf16),
            dma(()),
            dma((mp, chunks)),
            dma((mp,)),
            dma((mp,)),
            dma((dp,)),
            dma((dp,)),
            dma((dp,)),
            dma((dp,)),
        ],
        compiler_params=pltpu.CompilerParams(
            collective_id=0, has_side_effects=True, vmem_limit_bytes=56 * 1024 * 1024),
    )(counts, slot_plan, norm_gain.reshape(1, -1), queries, store_rows, key_weight, value_weight)


def solution(mesh):
    placed = (P("dp", "mp"), P(), P(None, "mp"), P(None, "mp"), P("dp", "mp"), P(), P("dp"))
    return jax.shard_map(
        functools.partial(local, mesh.shape["dp"], mesh.shape["mp"]),
        mesh=mesh, in_specs=placed, out_specs=P("dp", "mp"), check_vma=False
    )
```

```python
import functools

import jax
import jax.numpy as jnp
from jax import lax
from jax.experimental import pallas as pl
from jax.experimental.pallas import tpu as pltpu
from jax.sharding import PartitionSpec as P

HEAD_DIM = 64
MESH = pl.DeviceIdType.MESH

norm_eps = 1e-06
score_scale = 0.125
far_below = -1e30


def body(dims, counts, plan, gain, queries, rows_hbm, key_hbm, value_hbm, out,
         raw, scaled, wbuf, acc, kvb, sumsq, qbuf, part1, stat1, part2, stat2, part3, stat3,
         rows_sem, w_sem, rsend, rrecv, qsend, qrecv, send1, recv1, send2, recv2):
    dp, mp, inner_count, row_count, feats, cols, piece, width, questions, dec, passages = dims
    full = feats * mp
    pieces = feats // piece
    seq = row_count // passages
    groups = cols // width
    gheads = width // HEAD_DIM
    outer_count = dp // inner_count
    me = lax.axis_index("dp")
    core = lax.axis_index("mp")
    inner = lax.rem(me, inner_count)
    outer = lax.div(me, inner_count)
    weights = (key_hbm, value_hbm)

    def feature_span(k):
        return pl.ds(k * piece, piece)

    def own_copy(k):
        return pltpu.make_async_copy(
            rows_hbm.at[:, feature_span(k)], raw.at[0, :, feature_span(k)], rows_sem.at[k])

    def weight_copy(s, k, c):
        start = lax.rem(core + s, mp) * feats + k * piece
        return pltpu.make_async_copy(
            weights[c].at[pl.ds(pl.multiple_of(start, piece), piece), :],
            wbuf.at[s, k, c], w_sem.at[s, k, c])

    for k in range(pieces):
        own_copy(k).start()
        for c in range(2):
            weight_copy(0, k, c).start()

    barrier = pltpu.get_barrier_semaphore()
    for s in range(1, mp):
        pl.semaphore_signal(barrier, inc=1, device_id=(me, lax.rem(core + s, mp)), device_id_type=MESH)
    for j in range(1, dp):
        pl.semaphore_signal(barrier, inc=1, device_id=(lax.rem(me + j, dp), core), device_id_type=MESH)
    pl.semaphore_wait(barrier, dp - 1 + mp - 1)

    def row_copy(s, k):
        return pltpu.make_async_remote_copy(
            src_ref=rows_hbm.at[:, feature_span(k)], dst_ref=raw.at[s, :, feature_span(k)],
            send_sem=rsend.at[s, k], recv_sem=rrecv.at[s, k],
            device_id=(me, lax.rem(core + mp - s, mp)), device_id_type=MESH)

    for s in range(1, mp):
        for k in range(pieces):
            row_copy(s, k).start()
    query_copies = []
    for j in range(1, dp):
        query_copies.append(pltpu.make_async_remote_copy(
            src_ref=queries, dst_ref=qbuf.at[me], send_sem=qsend.at[j], recv_sem=qrecv.at[j],
            device_id=(lax.rem(me + j, dp), core), device_id_type=MESH))
        query_copies[-1].start()
    for s in range(1, mp):
        for k in range(pieces):
            for c in range(2):
                weight_copy(s, k, c).start()
    qbuf[me] = queries[...]

    row_step = 64

    def scale(s, k):
        start = lax.rem(core + s, mp) * feats + k * piece
        own_gain = gain[:, pl.ds(pl.multiple_of(start, piece), piece)].astype(jnp.float32)

        def step(i, carry):
            at = pl.ds(pl.multiple_of(i * row_step, row_step), row_step)
            x = raw[s, at, feature_span(k)].astype(jnp.float32)
            scaled[at, :] = (x * own_gain).astype(jnp.bfloat16)
            total = jnp.sum(x * x, axis=1, keepdims=True)
            if s + k > 0:
                total = total + sumsq[at, :]
            sumsq[at, :] = total
            return carry

        lax.fori_loop(0, row_count // row_step, step, 0)

    for s in range(mp):
        for k in range(pieces):
            if s == 0:
                own_copy(k).wait()
            else:
                row_copy(s, k).wait()
            scale(s, k)
            last = s == mp - 1 and k == pieces - 1
            if last:
                inv_rms = lax.rsqrt(sumsq[...] * (1.0 / full) + norm_eps)
            for c in range(2):
                weight_copy(s, k, c).wait()
                product = jnp.dot(scaled[...], wbuf[s, k, c], preferred_element_type=jnp.float32)
                if s + k > 0:
                    product = product + acc[c]
                if last:
                    kvb[c] = (product * inv_rms).astype(jnp.bfloat16)
                else:
                    acc[c] = product

    for copy in query_copies:
        copy.wait()

    slot = []
    for p in range(passages):
        plan_p = plan[p]

        def count(q, carry):
            end, total = carry
            end = end + counts[q]
            return end, total + jnp.where(end <= plan_p, 1, 0)

        found = lax.fori_loop(0, questions, count, (jnp.int32(0), jnp.int32(0)))[1]
        slot.append(jnp.minimum(found, questions - 1))

    tall = gheads * dec
    row_head = lax.broadcasted_iota(jnp.int32, (tall, width), 0) // dec
    col_head = lax.broadcasted_iota(jnp.int32, (tall, width), 1) // HEAD_DIM
    diagonal = row_head == col_head
    stat_row = lax.broadcasted_iota(jnp.int32, (tall, 128), 0) // dec
    stat_lane = lax.broadcasted_iota(jnp.int32, (tall, 128), 1)

    for p in range(passages):
        own_queries = qbuf[slot[p]].astype(jnp.float32)
        stats = jnp.zeros((dec, 128), jnp.float32)
        for g in range(groups):
            at = slice(g * width, (g + 1) * width)
            q = own_queries[:, at]
            q = jnp.where(diagonal, jnp.concatenate([q] * gheads, axis=0), 0.0).astype(jnp.bfloat16)
            k = kvb[0, p * seq:(p + 1) * seq, at]
            scores = lax.dot_general(q, k, (((1,), (1,)), ((), ())), preferred_element_type=jnp.float32) * score_scale
            level = jnp.max(scores, axis=1, keepdims=True)
            w = jnp.exp(scores - level)
            den = jnp.sum(w, axis=1, keepdims=True)
            v = kvb[1, p * seq:(p + 1) * seq, at]
            num = jnp.dot(w.astype(jnp.bfloat16), v, preferred_element_type=jnp.float32)
            mine = jnp.where(diagonal, num / den, 0.0)
            part1[inner, p, :, at] = jnp.sum(mine.reshape(gheads, dec, width), axis=0).astype(jnp.bfloat16)
            lse = jnp.broadcast_to(level + jnp.log(den), (tall, 128))
            put = stat_lane == stat_row + g * gheads
            stats = stats + jnp.sum(jnp.where(put, lse, 0.0).reshape(gheads, dec, 128), axis=0)
        stat1[inner, p, 0] = stats
        stat1[inner, p, 1] = jnp.full((dec, 128), slot[p].astype(jnp.float32))

    copies1 = []
    for j in range(1, inner_count):
        target = (outer * inner_count + lax.rem(inner + j, inner_count), core)
        for i, buf in enumerate((part1, stat1)):
            copies1.append(pltpu.make_async_remote_copy(
                src_ref=buf.at[inner], dst_ref=buf.at[inner], send_sem=send1.at[i, j], recv_sem=recv1.at[i, j],
                device_id=target, device_id_type=MESH))
            copies1[-1].start()

    pick_row = lax.rem(lax.broadcasted_iota(jnp.int32, (256, cols), 0), 128)
    pick_col = lax.broadcasted_iota(jnp.int32, (256, cols), 1) // HEAD_DIM
    pick = jnp.where(pick_row == pick_col, 1.0, 0.0).astype(jnp.bfloat16)

    def merge(lse, hit, parts):
        n = lse.shape[0]
        lse = jnp.where(hit, lse, far_below)
        level = jnp.max(lse, axis=0)
        w = jnp.where(hit, jnp.exp(lse - level[None]), 0.0)
        den = jnp.sum(w, axis=0)
        some = den > 0.0
        den = jnp.where(some, den, 1.0)
        share = (w / den[None]).reshape(n * dec, 128)
        high = share.astype(jnp.bfloat16)
        low = (share - high.astype(jnp.float32)).astype(jnp.bfloat16)
        wide = jnp.dot(jnp.concatenate([high, low], axis=1), pick, preferred_element_type=jnp.float32)
        merged = jnp.sum(wide.reshape(n, dec, cols) * parts, axis=0)
        return merged.astype(jnp.bfloat16), jnp.where(some, level + jnp.log(den), far_below)

    for copy in copies1:
        copy.wait()

    count1 = inner_count * passages
    lse1 = stat1[:, :, 0].reshape(count1, dec, 128)
    slots1 = stat1[:, :, 1].reshape(count1, dec, 128)
    parts1 = part1[...].astype(jnp.float32).reshape(count1, dec, cols)
    copies2 = []
    for j in list(range(1, outer_count)) + [0]:
        target_outer = lax.rem(outer + j, outer_count)
        dst = target_outer * inner_count + inner
        merged, lse = merge(lse1, slots1 == dst.astype(jnp.float32), parts1)
        if j == 0:
            part3[outer] = merged
            stat3[outer] = lse
            continue
        part2[j] = merged
        stat2[j] = lse
        for i, (source, sink) in enumerate(((part2, part3), (stat2, stat3))):
            copies2.append(pltpu.make_async_remote_copy(
                src_ref=source.at[j], dst_ref=sink.at[outer], send_sem=send2.at[i, j], recv_sem=recv2.at[i, j],
                device_id=(dst, core), device_id_type=MESH))
            copies2[-1].start()
    for copy in copies2:
        copy.wait()

    lse3 = stat3[...]
    out[...] = merge(lse3, lse3 > 0.5 * far_below, part3[...].astype(jnp.float32))[0]


def local(dp, mp, store_rows, norm_gain, key_weight, value_weight, queries, counts, slot_plan):
    row_count, feats = store_rows.shape
    cols = key_weight.shape[1]
    width = min(256, cols)
    piece = min(512, feats)
    pieces = feats // piece
    passages = slot_plan.shape[0]
    dec = queries.shape[0]
    questions = counts.shape[0]
    inner = 1
    while inner * inner < dp and dp % (2 * inner) == 0:
        inner *= 2
    outer = dp // inner
    dims = (dp, mp, inner, row_count, feats, cols, piece, width, questions, dec, passages)
    vmem = pl.BlockSpec(memory_space=pltpu.VMEM)
    smem = pl.BlockSpec(memory_space=pltpu.SMEM)
    hbm = pl.BlockSpec(memory_space=pl.ANY)
    bf16, f32 = jnp.bfloat16, jnp.float32
    dma = pltpu.SemaphoreType.DMA
    return pl.pallas_call(
        functools.partial(body, dims),
        out_shape=jax.ShapeDtypeStruct((dec, cols), bf16),
        in_specs=[smem, smem, vmem, vmem, hbm, hbm, hbm],
        out_specs=vmem,
        scratch_shapes=[
            pltpu.VMEM((mp, row_count, feats), bf16),
            pltpu.VMEM((row_count, piece), bf16),
            pltpu.VMEM((mp, pieces, 2, piece, cols), bf16),
            pltpu.VMEM((2, row_count, cols), f32),
            pltpu.VMEM((2, row_count, cols), bf16),
            pltpu.VMEM((row_count, 1), f32),
            pltpu.VMEM((dp, dec, cols), bf16),
            pltpu.VMEM((inner, passages, dec, cols), bf16),
            pltpu.VMEM((inner, passages, 2, dec, 128), f32),
            pltpu.VMEM((outer, dec, cols), bf16),
            pltpu.VMEM((outer, dec, 128), f32),
            pltpu.VMEM((outer, dec, cols), bf16),
            pltpu.VMEM((outer, dec, 128), f32),
            dma((pieces,)),
            dma((mp, pieces, 2)),
            dma((mp, pieces)),
            dma((mp, pieces)),
            dma((dp,)),
            dma((dp,)),
            dma((2, inner)),
            dma((2, inner)),
            dma((2, outer)),
            dma((2, outer)),
        ],
        compiler_params=pltpu.CompilerParams(
            collective_id=0, has_side_effects=True, vmem_limit_bytes=56 * 1024 * 1024),
    )(counts, slot_plan, norm_gain.reshape(1, -1), queries, store_rows, key_weight, value_weight)


def solution(mesh):
    placed = (P("dp", "mp"), P(), P(None, "mp"), P(None, "mp"), P("dp", "mp"), P(), P("dp"))
    return jax.shard_map(
        functools.partial(local, mesh.shape["dp"], mesh.shape["mp"]),
        mesh=mesh, in_specs=placed, out_specs=P("dp", "mp"), check_vma=False
    )
```

```python
import functools

import jax
import jax.numpy as jnp
from jax import lax
from jax.experimental import pallas as pl
from jax.experimental.pallas import tpu as pltpu
from jax.sharding import PartitionSpec as P

HEAD_DIM = 64
MESH = pl.DeviceIdType.MESH

norm_eps = 1e-06
score_scale = 0.125
far_below = -1e30


def body(dims, counts, plan, gain, queries, rows_hbm, key_hbm, value_hbm, out,
         raw, scaled, wbuf, acc, kvb, sumsq, qbuf, part1, stat1, part2, stat2, part3, stat3,
         rows_sem, w_sem, rsend, rrecv, qsend, qrecv, send1, recv1, send2, recv2):
    dp, mp, inner_count, row_count, feats, cols, piece, width, questions, dec, passages = dims
    full = feats * mp
    pieces = feats // piece
    seq = row_count // passages
    groups = cols // width
    gheads = width // HEAD_DIM
    outer_count = dp // inner_count
    me = lax.axis_index("dp")
    core = lax.axis_index("mp")
    inner = lax.rem(me, inner_count)
    outer = lax.div(me, inner_count)
    weights = (key_hbm, value_hbm)

    def feature_span(k):
        return pl.ds(k * piece, piece)

    def own_copy(k):
        return pltpu.make_async_copy(
            rows_hbm.at[:, feature_span(k)], raw.at[0, :, feature_span(k)], rows_sem.at[k])

    def weight_copy(s, k, c):
        start = lax.rem(core + s, mp) * feats + k * piece
        return pltpu.make_async_copy(
            weights[c].at[pl.ds(pl.multiple_of(start, piece), piece), :],
            wbuf.at[s, k, c], w_sem.at[s, k, c])

    for k in range(pieces):
        own_copy(k).start()
        for c in range(2):
            weight_copy(0, k, c).start()

    barrier = pltpu.get_barrier_semaphore()
    for s in range(1, mp):
        pl.semaphore_signal(barrier, inc=1, device_id=(me, lax.rem(core + s, mp)), device_id_type=MESH)
    for j in range(1, dp):
        pl.semaphore_signal(barrier, inc=1, device_id=(lax.rem(me + j, dp), core), device_id_type=MESH)
    pl.semaphore_wait(barrier, dp - 1 + mp - 1)

    def row_copy(s, k):
        return pltpu.make_async_remote_copy(
            src_ref=rows_hbm.at[:, feature_span(k)], dst_ref=raw.at[s, :, feature_span(k)],
            send_sem=rsend.at[s, k], recv_sem=rrecv.at[s, k],
            device_id=(me, lax.rem(core + mp - s, mp)), device_id_type=MESH)

    for s in range(1, mp):
        for k in range(pieces):
            row_copy(s, k).start()
    query_copies = []
    for j in range(1, dp):
        query_copies.append(pltpu.make_async_remote_copy(
            src_ref=queries, dst_ref=qbuf.at[me], send_sem=qsend.at[j], recv_sem=qrecv.at[j],
            device_id=(lax.rem(me + j, dp), core), device_id_type=MESH))
        query_copies[-1].start()
    for s in range(1, mp):
        for k in range(pieces):
            for c in range(2):
                weight_copy(s, k, c).start()
    qbuf[me] = queries[...]

    row_step = 64

    def scale(s, k):
        start = lax.rem(core + s, mp) * feats + k * piece
        own_gain = gain[pl.ds(pl.multiple_of(start, piece), piece)].astype(jnp.float32).reshape(1, piece)

        def step(i, carry):
            at = pl.ds(pl.multiple_of(i * row_step, row_step), row_step)
            x = raw[s, at, feature_span(k)].astype(jnp.float32)
            scaled[at, :] = (x * own_gain).astype(jnp.bfloat16)
            square = x * x
            total = square[:, :128]
            for lanes in range(128, piece, 128):
                total = total + square[:, lanes:lanes + 128]
            if s + k > 0:
                total = total + sumsq[at, :]
            sumsq[at, :] = total
            return carry

        lax.fori_loop(0, row_count // row_step, step, 0)

    for s in range(mp):
        for k in range(pieces):
            if s == 0:
                own_copy(k).wait()
            else:
                row_copy(s, k).wait()
            scale(s, k)
            last = s == mp - 1 and k == pieces - 1
            if last:
                inv_rms = lax.rsqrt(jnp.sum(sumsq[...], axis=1, keepdims=True) * (1.0 / full) + norm_eps)
            for c in range(2):
                weight_copy(s, k, c).wait()
                product = jnp.dot(scaled[...], wbuf[s, k, c], preferred_element_type=jnp.float32)
                if s + k > 0:
                    product = product + acc[c]
                if last:
                    kvb[c] = (product * inv_rms).astype(jnp.bfloat16)
                else:
                    acc[c] = product

    for copy in query_copies:
        copy.wait()

    slot = []
    for p in range(passages):
        plan_p = plan[p]

        def count(q, carry):
            end, total = carry
            end = end + counts[q]
            return end, total + jnp.where(end <= plan_p, 1, 0)

        found = lax.fori_loop(0, questions, count, (jnp.int32(0), jnp.int32(0)))[1]
        slot.append(jnp.minimum(found, questions - 1))

    tall = gheads * dec
    row_head = lax.broadcasted_iota(jnp.int32, (tall, width), 0) // dec
    col_head = lax.broadcasted_iota(jnp.int32, (tall, width), 1) // HEAD_DIM
    diagonal = row_head == col_head
    stat_row = lax.broadcasted_iota(jnp.int32, (tall, 128), 0) // dec
    stat_lane = lax.broadcasted_iota(jnp.int32, (tall, 128), 1)

    for p in range(passages):
        own_queries = qbuf[slot[p]].astype(jnp.float32)
        stats = jnp.zeros((dec, 128), jnp.float32)
        for g in range(groups):
            at = slice(g * width, (g + 1) * width)
            q = own_queries[:, at]
            q = jnp.where(diagonal, jnp.concatenate([q] * gheads, axis=0), 0.0).astype(jnp.bfloat16)
            k = kvb[0, p * seq:(p + 1) * seq, at]
            scores = lax.dot_general(q, k, (((1,), (1,)), ((), ())), preferred_element_type=jnp.float32) * score_scale
            level = jnp.max(scores, axis=1, keepdims=True)
            w = jnp.exp(scores - level)
            den = jnp.sum(w, axis=1, keepdims=True)
            v = kvb[1, p * seq:(p + 1) * seq, at]
            num = jnp.dot(w.astype(jnp.bfloat16), v, preferred_element_type=jnp.float32)
            mine = jnp.where(diagonal, num / den, 0.0)
            part1[inner, p, :, at] = jnp.sum(mine.reshape(gheads, dec, width), axis=0).astype(jnp.bfloat16)
            lse = jnp.broadcast_to(level + jnp.log(den), (tall, 128))
            put = stat_lane == stat_row + g * gheads
            stats = stats + jnp.sum(jnp.where(put, lse, 0.0).reshape(gheads, dec, 128), axis=0)
        stat1[inner, p, 0] = stats
        stat1[inner, p, 1] = jnp.full((dec, 128), slot[p].astype(jnp.float32))

    copies1 = []
    for j in range(1, inner_count):
        target = (outer * inner_count + lax.rem(inner + j, inner_count), core)
        for i, buf in enumerate((part1, stat1)):
            copies1.append(pltpu.make_async_remote_copy(
                src_ref=buf.at[inner], dst_ref=buf.at[inner], send_sem=send1.at[i, j], recv_sem=recv1.at[i, j],
                device_id=target, device_id_type=MESH))
            copies1[-1].start()

    pick_row = lax.rem(lax.broadcasted_iota(jnp.int32, (256, cols), 0), 128)
    pick_col = lax.broadcasted_iota(jnp.int32, (256, cols), 1) // HEAD_DIM
    pick = jnp.where(pick_row == pick_col, 1.0, 0.0).astype(jnp.bfloat16)

    def merge(lse, hit, parts):
        n = lse.shape[0]
        lse = jnp.where(hit, lse, far_below)
        level = jnp.max(lse, axis=0)
        w = jnp.where(hit, jnp.exp(lse - level[None]), 0.0)
        den = jnp.sum(w, axis=0)
        some = den > 0.0
        den = jnp.where(some, den, 1.0)
        share = (w / den[None]).reshape(n * dec, 128)
        high = share.astype(jnp.bfloat16)
        low = (share - high.astype(jnp.float32)).astype(jnp.bfloat16)
        wide = jnp.dot(jnp.concatenate([high, low], axis=1), pick, preferred_element_type=jnp.float32)
        merged = jnp.sum(wide.reshape(n, dec, cols) * parts, axis=0)
        return merged.astype(jnp.bfloat16), jnp.where(some, level + jnp.log(den), far_below)

    for copy in copies1:
        copy.wait()

    count1 = inner_count * passages
    lse1 = stat1[:, :, 0].reshape(count1, dec, 128)
    slots1 = stat1[:, :, 1].reshape(count1, dec, 128)
    parts1 = part1[...].astype(jnp.float32).reshape(count1, dec, cols)
    copies2 = []
    for j in list(range(1, outer_count)) + [0]:
        target_outer = lax.rem(outer + j, outer_count)
        dst = target_outer * inner_count + inner
        merged, lse = merge(lse1, slots1 == dst.astype(jnp.float32), parts1)
        if j == 0:
            part3[outer] = merged
            stat3[outer] = lse
            continue
        part2[j] = merged
        stat2[j] = lse
        for i, (source, sink) in enumerate(((part2, part3), (stat2, stat3))):
            copies2.append(pltpu.make_async_remote_copy(
                src_ref=source.at[j], dst_ref=sink.at[outer], send_sem=send2.at[i, j], recv_sem=recv2.at[i, j],
                device_id=(dst, core), device_id_type=MESH))
            copies2[-1].start()
    for copy in copies2:
        copy.wait()

    lse3 = stat3[...]
    out[...] = merge(lse3, lse3 > 0.5 * far_below, part3[...].astype(jnp.float32))[0]


def local(dp, mp, store_rows, norm_gain, key_weight, value_weight, queries, counts, slot_plan):
    row_count, feats = store_rows.shape
    cols = key_weight.shape[1]
    width = min(256, cols)
    piece = min(512, feats)
    pieces = feats // piece
    passages = slot_plan.shape[0]
    dec = queries.shape[0]
    questions = counts.shape[0]
    inner = 1
    while inner * inner < dp and dp % (2 * inner) == 0:
        inner *= 2
    outer = dp // inner
    dims = (dp, mp, inner, row_count, feats, cols, piece, width, questions, dec, passages)
    vmem = pl.BlockSpec(memory_space=pltpu.VMEM)
    smem = pl.BlockSpec(memory_space=pltpu.SMEM)
    hbm = pl.BlockSpec(memory_space=pl.ANY)
    bf16, f32 = jnp.bfloat16, jnp.float32
    dma = pltpu.SemaphoreType.DMA
    return pl.pallas_call(
        functools.partial(body, dims),
        out_shape=jax.ShapeDtypeStruct((dec, cols), bf16),
        in_specs=[smem, smem, vmem, vmem, hbm, hbm, hbm],
        out_specs=vmem,
        scratch_shapes=[
            pltpu.VMEM((mp, row_count, feats), bf16),
            pltpu.VMEM((row_count, piece), bf16),
            pltpu.VMEM((mp, pieces, 2, piece, cols), bf16),
            pltpu.VMEM((2, row_count, cols), f32),
            pltpu.VMEM((2, row_count, cols), bf16),
            pltpu.VMEM((row_count, 128), f32),
            pltpu.VMEM((dp, dec, cols), bf16),
            pltpu.VMEM((inner, passages, dec, cols), bf16),
            pltpu.VMEM((inner, passages, 2, dec, 128), f32),
            pltpu.VMEM((outer, dec, cols), bf16),
            pltpu.VMEM((outer, dec, 128), f32),
            pltpu.VMEM((outer, dec, cols), bf16),
            pltpu.VMEM((outer, dec, 128), f32),
            dma((pieces,)),
            dma((mp, pieces, 2)),
            dma((mp, pieces)),
            dma((mp, pieces)),
            dma((dp,)),
            dma((dp,)),
            dma((2, inner)),
            dma((2, inner)),
            dma((2, outer)),
            dma((2, outer)),
        ],
        compiler_params=pltpu.CompilerParams(
            collective_id=0, has_side_effects=True, vmem_limit_bytes=56 * 1024 * 1024),
    )(counts, slot_plan, norm_gain, queries, store_rows, key_weight, value_weight)


def solution(mesh):
    placed = (P("dp", "mp"), P(), P(None, "mp"), P(None, "mp"), P("dp", "mp"), P(), P("dp"))
    return jax.shard_map(
        functools.partial(local, mesh.shape["dp"], mesh.shape["mp"]),
        mesh=mesh, in_specs=placed, out_specs=P("dp", "mp"), check_vma=False
    )
```
